32 devices in a mesh: rep: 2 (over y), seq: 8 (over z, x), head: 2 (over core).
Axes of the slice: x: 2, y: 2, z: 4, core: 2. Of those that a mesh axis runs over, the one named last changes fastest.
Arguments:
- queries: bfloat16 [1024, 4096], P(('rep', 'seq'), 'head'), parts along dimension 0, may hold values from -5 to 5
- keys: bfloat16 [1024, 512], P(('rep', 'seq'), 'head'), parts along dimension 0, may hold values from -5 to 5
- values: bfloat16 [1024, 512], P(('rep', 'seq'), 'head'), parts along dimension 0, may hold values from -5 to 5
- key_steer_direction: bfloat16 [512], P('head'), may hold values from -3 to 3
- value_steer_direction: bfloat16 [512], P('head'), may hold values from -6 to 6
- strength: float32 [2], P('rep'), parts along dimension 0, may hold values from 0.5 to 1.5
- block_order: int32 [32], P('rep'), parts along dimension 0, may hold values from 0 to 15, as said below
- steer_pos: int32 [256], P('rep'), parts along dimension 0, may hold values from 0 to 511
- target: bfloat16 [1024, 4096], P(('rep', 'seq'), 'head'), parts along dimension 0, may hold values from -6 to 6
Outputs:
- attn_out: bfloat16 [1024, 4096], P(('rep', 'seq'), 'head'), parts along dimension 0
- attn_tangent: bfloat16 [1024, 4096], P(('rep', 'seq'), 'head'), parts along dimension 0
- sensitivity: float32 [2], P('rep'), parts along dimension 0
The draws below stay inside these ranges and needn't reach their ends.
There are 2 independent parts, one for each index of `rep`. The reference program is written for one: setup_inputs(seed, part) draws one part's arguments, and reference() takes and returns one part's arrays. A program takes and returns all parts, laid end to end along the dimension named above; an argument that names none is the same for every part. Nothing has to cross between parts.
Inputs may be any that keep to these rules, and one draw needn't show every extreme that they name: `block_order`: for each d below 8, stored blocks 2 d and 2 d + 1 hold the prompt blocks d and 2 * 8 - 1 - d, in either order.
All inputs are finite; a program needn't handle non-finite values.
Results may differ from the reference program's by a relative error of at most 0.0093.
Values may be sent and summed in bfloat16 or wider, within the bound.
A program may use at most 64 MiB of HBM per device.

```python
import math
import jax
import jax.numpy as jnp
from jax import lax

HQ = 32
KEY_VALUE_HEADS = 4
HEAD_WIDTH = 128
PROMPT_TOKENS = 512
BLK = 32
GQ = 8
NSTEER = 128


def draw_block_order(key, part):
    block_count = PROMPT_TOKENS // BLK
    half_count = block_count // 2
    early = jnp.arange(half_count, dtype=jnp.int32)
    flips = jax.random.randint(jax.random.fold_in(key, 31), (half_count,), 0, 2).astype(jnp.int32)
    first = jnp.where(flips == 1, block_count - 1 - early, early)
    second = block_count - 1 - first
    return jnp.stack([first, second], axis=1).reshape(block_count).astype(jnp.int32)


def draw_queries(key, part):
    random_base_key = jax.random.fold_in(key, 11)
    sampled_arrays = jax.random.normal(random_base_key, (PROMPT_TOKENS, HQ * HEAD_WIDTH), jnp.float32) * 2.4
    sampled_arrays = jnp.clip(sampled_arrays, -5.0, 5.0)
    return sampled_arrays.astype(jnp.bfloat16)


def draw_keys(key, part):
    random_base_key = jax.random.fold_in(key, 21)
    sampled_arrays = jax.random.normal(random_base_key, (PROMPT_TOKENS, KEY_VALUE_HEADS * HEAD_WIDTH), jnp.float32)
    sampled_arrays = jnp.clip(sampled_arrays, -5.0, 5.0)
    return sampled_arrays.astype(jnp.bfloat16)


def place_ends(entries, rng, least, top_value):
    index_at = [jax.random.randint(jax.random.fold_in(rng, axis), (), 0, length) for axis, length in enumerate(entries.shape)]
    widest = entries.shape.index(max(entries.shape))
    neighbour = index_at[:widest] + [(index_at[widest] + 1) % entries.shape[widest]] + index_at[widest + 1:]
    return entries.at[tuple(index_at)].set(least).at[tuple(neighbour)].set(top_value)


def block_scale(rng, extent, pieces, low, high):
    gain, own = 1.0, jax.random.fold_in(rng, 6)
    for dim, parts in pieces:
        heights = jnp.exp(jax.random.uniform(jax.random.fold_in(own, dim), (parts,), jnp.float32, low / len(pieces), high / len(pieces)))
        gain = gain * jnp.repeat(heights, extent[dim] // parts).reshape([-1 if axis == dim else 1 for axis in range(len(extent))])
    return gain


def gaussian(rng, shape, width, limit, split=(), kind=jnp.bfloat16):
    gain = block_scale(rng, shape, split, -0.22, 0.18) if split else 1.0
    result = jax.random.normal(rng, shape, jnp.float32) * width * gain
    return jnp.minimum(jnp.maximum(result, -limit), limit).astype(kind)


def setup_inputs(seed: int = 0, part: int = 0) -> dict:
    seeds = jax.random.split(jax.random.key(seed), 10)
    own_keys = jax.random.split(jax.random.fold_in(seeds[9], part), 10)
    queries = draw_queries(jax.random.fold_in(jax.random.fold_in(seeds[9], part), 71), part)
    keys = draw_keys(jax.random.fold_in(jax.random.fold_in(seeds[9], part), 71), part)
    values = gaussian(own_keys[2], (PROMPT_TOKENS, KEY_VALUE_HEADS * HEAD_WIDTH), 1.0, 5.0, ((0, 8), (1, 2)))
    key_steer_direction = gaussian(seeds[3], (KEY_VALUE_HEADS * HEAD_WIDTH,), 0.5, 3.0, ((0, 2),))
    value_steer_direction = gaussian(seeds[4], (KEY_VALUE_HEADS * HEAD_WIDTH,), 1.5, 6.0, ((0, 2),))
    strength = jnp.clip(jax.random.uniform(own_keys[5], (1,), jnp.float32, 0.5, 1.5), 0.5, 1.5)
    block_order = draw_block_order(jax.random.fold_in(jax.random.fold_in(seeds[9], part), 71), part)
    steer_pos = place_ends(jax.random.randint(own_keys[7], (NSTEER,), 0, PROMPT_TOKENS), jax.random.fold_in(own_keys[7], 1), 0, PROMPT_TOKENS - 1).astype(jnp.int32)
    target = gaussian(own_keys[8], (PROMPT_TOKENS, HQ * HEAD_WIDTH), 1.0, 6.0, ((0, 8), (1, 2)))
    return {"queries": queries, "keys": keys, "values": values, "key_steer_direction": key_steer_direction, "value_steer_direction": value_steer_direction, "strength": strength, "block_order": block_order, "steer_pos": steer_pos, "target": target}


def reference(queries, keys, values, key_steer_direction, value_steer_direction, strength, block_order, steer_pos, target):
    inverse = 1.0 / math.sqrt(HEAD_WIDTH)
    stored = jnp.arange(PROMPT_TOKENS, dtype=jnp.int32)
    position = block_order[stored // BLK] * BLK + stored % BLK
    flagged = jnp.zeros((PROMPT_TOKENS,), jnp.float32).at[steer_pos].set(1.0)
    causal_mask = flagged[position]
    steer_strength = strength[0]
    key_direction = key_steer_direction.astype(jnp.float32).reshape(KEY_VALUE_HEADS, HEAD_WIDTH)
    value_direction = value_steer_direction.astype(jnp.float32).reshape(KEY_VALUE_HEADS, HEAD_WIDTH)
    steered_keys = (keys.astype(jnp.float32).reshape(PROMPT_TOKENS, KEY_VALUE_HEADS, HEAD_WIDTH) + (steer_strength * causal_mask)[:, None, None] * key_direction[None]).astype(jnp.bfloat16)
    steered_values = (values.astype(jnp.float32).reshape(PROMPT_TOKENS, KEY_VALUE_HEADS, HEAD_WIDTH) + (steer_strength * causal_mask)[:, None, None] * value_direction[None]).astype(jnp.bfloat16)
    values_masked = (causal_mask[:, None, None] * steered_values.astype(jnp.float32)).astype(jnp.bfloat16)
    keys_heads = jnp.transpose(steered_keys, (1, 0, 2))
    values_heads = jnp.transpose(jnp.concatenate([steered_values, values_masked], axis=2), (1, 0, 2))
    query_heads = jnp.transpose(queries.reshape(PROMPT_TOKENS, HQ, HEAD_WIDTH), (1, 0, 2))
    key_steer_vector = key_steer_direction.reshape(KEY_VALUE_HEADS, HEAD_WIDTH)
    visible = position[None, :] <= position[:, None]

    def one_head(inputs):
        query_one, head_id = inputs
        group_id = head_id // GQ
        key_one = lax.dynamic_index_in_dim(keys_heads, group_id, 0, keepdims=False)
        value_one = lax.dynamic_index_in_dim(values_heads, group_id, 0, keepdims=False)
        direction = lax.dynamic_index_in_dim(key_steer_vector, group_id, 0, keepdims=False)
        value_add = lax.dynamic_index_in_dim(value_direction, group_id, 0, keepdims=False)
        scores = jnp.dot(query_one, key_one.T, preferred_element_type=jnp.float32) * inverse
        scores = jnp.where(visible, scores, -jnp.inf)
        largest = lax.optimization_barrier(jnp.max(scores, axis=1, keepdims=True))
        weights_raw = jnp.where(visible, jnp.exp(scores - largest), 0.0)
        totals = lax.optimization_barrier(jnp.sum(weights_raw, axis=1))
        weights_low = weights_raw.astype(jnp.bfloat16)
        summed = jnp.dot(weights_low, value_one, preferred_element_type=jnp.float32)
        output = summed[:, :HEAD_WIDTH] / totals[:, None]
        moment = summed[:, HEAD_WIDTH:]
        massed = lax.optimization_barrier(jnp.sum(weights_low.astype(jnp.float32) * causal_mask[None, :], axis=1))
        coefficient = jnp.dot(query_one, direction, preferred_element_type=jnp.float32) * inverse
        tangent = coefficient[:, None] * (moment - massed[:, None] * output) / totals[:, None] + (massed / totals)[:, None] * value_add[None, :]
        return (output, tangent)
    head_ids = jnp.arange(HQ, dtype=jnp.int32)
    outputs_all, tangents_all = lax.map(one_head, (query_heads, head_ids))
    outputs_flat = jnp.transpose(outputs_all, (1, 0, 2)).reshape(PROMPT_TOKENS, HQ * HEAD_WIDTH)
    tangents_flat = jnp.transpose(tangents_all, (1, 0, 2)).reshape(PROMPT_TOKENS, HQ * HEAD_WIDTH)
    sensitivity = (jnp.sum(tangents_flat * target.astype(jnp.float32)) / math.sqrt(PROMPT_TOKENS * HQ * HEAD_WIDTH)).reshape(1)
    return (outputs_flat.astype(jnp.bfloat16), tangents_flat.astype(jnp.bfloat16), sensitivity)
```

```python
import functools
import math

import jax
import jax.numpy as jnp
from jax import lax
from jax.experimental import pallas as pl
from jax.experimental.pallas import tpu as pltpu
from jax.sharding import PartitionSpec as P

HEAD_WIDTH = 128
MESH = pl.DeviceIdType.MESH
LANES = 128
MASKED = -1e30


def repeat(low, high, step):
    if high - low <= 16:
        for i in range(low, high):
            step(i)
    else:
        lax.fori_loop(low, high, lambda i, c: (step(i), c)[1], 0)


def kernel(
    n,
    heads,
    span,
    order_hbm,
    strength_hbm,
    steer_hbm,
    kdir_hbm,
    vdir_hbm,
    keys_hbm,
    values_hbm,
    queries_hbm,
    target_hbm,
    out_hbm,
    tan_hbm,
    sens_hbm,
    order_ref,
    strength_ref,
    steer_ref,
    kdir_ref,
    vdir_ref,
    keys_ref,
    values_ref,
    kv,
    qbuf,
    tbuf,
    marks,
    score,
    weight,
    state,
    acc,
    parts,
    local_sem,
    early_send,
    early_recv,
    late_send,
    late_recv,
    part_send,
    part_recv,
):
    me = lax.axis_index("seq")
    my_head = lax.axis_index("head")
    rows, q_cols = qbuf.shape
    blk = rows // 2
    total_rows = kv.shape[0]
    kv_cols = keys_ref.shape[1]
    kv_local = kv_cols // HEAD_WIDTH
    grouping = q_cols // HEAD_WIDTH // kv_local
    width = grouping * rows
    inverse = 1.0 / math.sqrt(HEAD_WIDTH)
    exponent = inverse * math.log2(math.e)
    chunks = total_rows // span

    barrier = pltpu.get_barrier_semaphore()

    side = lax.rem(me, 2)
    pair = me + 1 - 2 * side
    mate = 1 - 2 * side
    seat = me // 2
    seats = n // 2

    def greet(seq, head):
        pl.semaphore_signal(
            barrier, inc=1, device_id={"seq": seq, "head": head}, device_id_type=MESH
        )

    repeat(1, seats, lambda k: greet(lax.rem(me + 2 * k, n), my_head))
    greet(pair, my_head)
    repeat(1, heads, lambda k: greet(me, lax.rem(my_head + k, heads)))

    fetched = []
    for i, (source, held) in enumerate(
        (
            (keys_hbm, keys_ref),
            (values_hbm, values_ref),
            (steer_hbm, steer_ref),
            (order_hbm, order_ref),
            (strength_hbm, strength_ref),
            (kdir_hbm, kdir_ref),
            (vdir_hbm, vdir_ref),
            (queries_hbm, qbuf),
            (target_hbm, tbuf),
        )
    ):
        fetched.append(pltpu.make_async_copy(source, held, local_sem.at[2 + i]))
        fetched[-1].start()
    q_copy, t_copy = fetched[7:]

    def clear(owner):
        @pl.when(owner < me)
        def _():
            start = pl.multiple_of((2 * n - 1 - owner) * blk, blk)
            kv[pl.ds(start, blk), :] = jnp.zeros((blk, 2 * kv_cols), kv.dtype)

    repeat(0, n - 1, clear)

    for copy in fetched[:7]:
        copy.wait()
    steer_count = steer_ref.shape[1]

    def marked(first, count):
        place = first + lax.broadcasted_iota(jnp.int32, (count, LANES), 0)
        hit = jnp.zeros((count, LANES), jnp.float32)
        for c in range(0, steer_count, LANES):
            listed = steer_ref[:, c : c + LANES]
            hit = jnp.where(place == listed, 1.0, hit)
        return jnp.max(hit, axis=1, keepdims=True)

    order_first = order_ref[2 * me]
    order_second = order_ref[2 * me + 1]
    early_start = pl.multiple_of(me * blk, blk)
    late_start = pl.multiple_of((2 * n - 1 - me) * blk, blk)
    strength = strength_ref[0]
    first_is_early = jnp.full((blk, kv_cols), order_first, jnp.int32) < n
    for source, direction, column in ((keys_ref, kdir_ref, 0), (values_ref, vdir_ref, kv_cols)):
        first = source[0:blk, :].astype(jnp.float32)
        second = source[blk:rows, :].astype(jnp.float32)
        step = direction[...].astype(jnp.float32).reshape(1, kv_cols)
        early = jnp.where(first_is_early, first, second)
        late = jnp.where(first_is_early, second, first)
        for block, start in ((early, early_start), (late, late_start)):
            moved = block + (strength * marked(start, blk)) * step
            kv[pl.ds(start, blk), column : column + kv_cols] = moved.astype(jnp.bfloat16)

    pl.semaphore_wait(barrier, seats + heads - 1)

    def block_copy(owner, late, device, lane):
        start = (2 * n - 1 - owner) * blk if late else owner * blk
        place_rows = kv.at[pl.ds(pl.multiple_of(start, blk), blk), :]
        sends, lands = (late_send, late_recv) if late else (early_send, early_recv)
        return pltpu.make_async_remote_copy(
            src_ref=place_rows,
            dst_ref=place_rows,
            send_sem=sends.at[lane],
            recv_sem=lands.at[owner],
            device_id={"seq": device},
            device_id_type=MESH,
        )

    def both_ways(step):
        def near(k):
            @pl.when(seat >= k)
            def _():
                step(me - 2 * k, True)

            @pl.when(seat + k < seats)
            def _():
                step(me + 2 * k, False)

        repeat(1, seats, near)

    block_copy(me, False, pair, pair).start()

    @pl.when(side == 1)
    def _():
        block_copy(me, True, pair, pair).start()

    def send(peer, lower):
        block_copy(me, False, peer, peer).start()
        if lower:
            block_copy(me, True, peer, peer).start()

    both_ways(send)

    def mark_rows(c):
        start = c * span
        if not isinstance(c, int):
            start = pl.multiple_of(start, span)
        marks[pl.ds(start, span), :] = jnp.broadcast_to(
            marked(start, span), (span, LANES)
        ).astype(jnp.bfloat16)

    repeat(0, chunks, mark_rows)

    row = lax.broadcasted_iota(jnp.int32, (rows, span), 0)
    column = lax.broadcasted_iota(jnp.int32, (rows, span), 1)
    own_block = jnp.where(row < blk, order_first, order_second)
    place = own_block * blk + lax.rem(row, blk)

    q_copy.wait()
    coefs = []
    for g in range(kv_local):
        query = jnp.concatenate(
            [
                qbuf[:, (g * grouping + h) * LANES : (g * grouping + h + 1) * LANES]
                for h in range(grouping)
            ],
            axis=0,
        )
        spread = jnp.broadcast_to(kdir_ref[g * LANES : (g + 1) * LANES].reshape(1, LANES), (LANES, LANES))
        coef = lax.dot_general(
            query, spread, (((1,), (1,)), ((), ())), preferred_element_type=jnp.float32
        )
        coefs.append((query, coef * inverse))

    def relay(peer, lower):
        block_copy(peer, False, pair, peer + mate).wait_recv()
        block_copy(peer, False, pair, peer + mate).start()
        if not lower:
            block_copy(peer, True, pair, peer + mate).wait_recv()
            block_copy(peer, True, pair, peer + mate).start()

    both_ways(relay)

    def arrive(peer, lower):
        block_copy(peer + mate, False, pair, peer).wait_recv()
        if not lower:
            block_copy(peer + mate, True, pair, peer).wait_recv()

    block_copy(pair, False, pair, pair).wait_recv()

    @pl.when(side == 0)
    def _():
        block_copy(pair, True, pair, pair).wait_recv()

    both_ways(arrive)

    def attend(g, c, start, fresh):
        query = coefs[g][0]
        key = kv[pl.ds(start, span), g * LANES : (g + 1) * LANES]
        score[...] = lax.dot_general(
            query, key, (((1,), (1,)), ((), ())), preferred_element_type=jnp.float32
        )
        visible = (column + start) <= place
        for h in range(grouping):
            part = slice(h * rows, (h + 1) * rows)
            scores = jnp.where(visible, score[part, :], MASKED)
            largest = jnp.max(scores, axis=1, keepdims=True)
            if not fresh:
                before = state[g, 0, part, :][:, 0:1]
                largest = jnp.maximum(before, largest)
            raw = jnp.exp2((scores - largest) * exponent)
            if not fresh:
                raw = jnp.where(visible, raw, 0.0)
            total = jnp.sum(raw, axis=1, keepdims=True)
            if not fresh:
                scale = jnp.exp2((before - largest) * exponent)
                total = total + scale * state[g, 1, part, :][:, 0:1]
                state[g, 0, part, :] = jnp.broadcast_to(largest, (rows, LANES))
                acc[g, part, :] = acc[g, part, :] * scale
            state[g, 1, part, :] = jnp.broadcast_to(total, (rows, LANES))
            weight[part, :] = raw.astype(jnp.bfloat16)
        mark = marks[pl.ds(start, span), :]
        value = kv[pl.ds(start, span), kv_cols + g * LANES : kv_cols + (g + 1) * LANES]
        stacked = jnp.concatenate([value, value * mark, mark], axis=1)
        found = jnp.dot(weight[...], stacked, preferred_element_type=jnp.float32)
        if fresh:
            acc[g] = found
        else:
            acc[g] = acc[g] + found

    if chunks == 1:
        for g in range(kv_local):
            attend(g, 0, 0, True)
    else:
        state[:, 0] = jnp.full_like(state[:, 0], MASKED)
        state[:, 1] = jnp.zeros_like(state[:, 1])
        acc[...] = jnp.zeros_like(acc)

        def chunk(c, carry):
            for g in range(kv_local):
                attend(g, c, pl.multiple_of(c * span, span), False)
            return carry

        lax.fori_loop(0, chunks, chunk, 0)

    t_copy.wait()
    inner = jnp.zeros((rows, LANES), jnp.float32)
    for g in range(kv_local):
        direction = vdir_ref[g * LANES : (g + 1) * LANES].astype(jnp.float32).reshape(1, LANES)
        for h in range(grouping):
            part = slice(h * rows, (h + 1) * rows)
            lanes = slice((g * grouping + h) * LANES, (g * grouping + h + 1) * LANES)
            share = 1.0 / state[g, 1, part, :]
            primal = acc[g, part, 0:LANES] * share
            moment = acc[g, part, LANES : 2 * LANES]
            mass = acc[g, part, 2 * LANES : 3 * LANES]
            coef = coefs[g][1][part, :]
            deriv = (coef * (moment - mass * primal) + mass * direction) * share
            inner = inner + deriv * tbuf[:, lanes].astype(jnp.float32)
            out_hbm[:, lanes] = primal.astype(jnp.bfloat16)
            tan_hbm[:, lanes] = deriv.astype(jnp.bfloat16)

    parts[n + my_head] = jnp.sum(inner, axis=0, keepdims=True)

    def part_copy(seq, head, slot, lane):
        return pltpu.make_async_remote_copy(
            src_ref=parts.at[slot],
            dst_ref=parts.at[slot],
            send_sem=part_send.at[lane],
            recv_sem=part_recv.at[slot],
            device_id={"seq": seq, "head": head},
            device_id_type=MESH,
        )

    def head_out(k):
        head = lax.rem(my_head + k, heads)
        return part_copy(me, head, n + my_head, n + head)

    def head_in(k):
        head = lax.rem(my_head + k, heads)
        return part_copy(me, head, n + head, n + head)

    def seq_out(k):
        seq = lax.rem(me + k, n)
        return part_copy(seq, my_head, me, seq)

    def seq_in(k):
        seq = lax.rem(me + k, n)
        return part_copy(seq, my_head, seq, seq)

    repeat(1, heads, lambda k: head_out(k).start())
    repeat(1, heads, lambda k: head_in(k).wait_recv())
    row_sum = parts[n]
    for i in range(1, heads):
        row_sum = row_sum + parts[n + i]
    parts[me] = row_sum
    repeat(1, n, lambda k: seq_out(k).start())
    repeat(1, n, lambda k: seq_in(k).wait_recv())
    if n <= 16:
        whole = parts[0]
        for i in range(1, n):
            whole = whole + parts[i]
    else:
        whole = lax.fori_loop(1, n, lambda i, t: t + parts[i], parts[0])
    scale = 1.0 / math.sqrt(total_rows * q_cols * heads)
    sens_hbm[...] = jnp.broadcast_to(jnp.sum(whole, axis=1, keepdims=True) * scale, (1, LANES))

    block_copy(me, False, pair, pair).wait_send()

    @pl.when(side == 1)
    def _():
        block_copy(me, True, pair, pair).wait_send()

    def sent(peer, lower):
        block_copy(me, False, peer, peer).wait_send()
        block_copy(peer, False, pair, peer + mate).wait_send()
        block_copy(me if lower else peer, True, pair, peer if lower else peer + mate).wait_send()

    both_ways(sent)
    repeat(1, heads, lambda k: head_out(k).wait_send())
    repeat(1, n, lambda k: seq_out(k).wait_send())


def store(primal, deriv, sens, primal_out, deriv_out, sens_out, one, sem):
    puts = [
        pltpu.make_async_copy(primal, primal_out, sem.at[0]),
        pltpu.make_async_copy(deriv, deriv_out, sem.at[1]),
        pltpu.make_async_copy(one, sens_out, sem.at[2]),
    ]
    puts[0].start()
    puts[1].start()
    one[...] = sens[0, 0:1]
    puts[2].start()
    for put in puts:
        put.wait()


def body(queries, keys, values, kdir, vdir, strength, order, steer, target):
    n = lax.axis_size("seq")
    heads = lax.axis_size("head")
    rows, q_cols = queries.shape
    kv_cols = keys.shape[1]
    kv_local = kv_cols // HEAD_WIDTH
    width = rows * (q_cols // kv_cols)
    total_rows = rows * n
    span = min(512, total_rows)
    anywhere = pl.BlockSpec(memory_space=pltpu.HBM)
    dma = pltpu.SemaphoreType.DMA
    vm = pl.BlockSpec(memory_space=pltpu.VMEM)
    outs = tuple(
        pl.pallas_call(
            functools.partial(kernel, n, heads, span),
            name="attend",
            out_shape=(
                pltpu.VMEM((rows, q_cols), jnp.bfloat16),
                pltpu.VMEM((rows, q_cols), jnp.bfloat16),
                pltpu.VMEM((1, LANES), jnp.float32),
            ),
            in_specs=[anywhere] * 9,
            out_specs=(vm,) * 3,
            scratch_shapes=[
                pltpu.SMEM(order.shape, jnp.int32),
                pltpu.SMEM(strength.shape, jnp.float32),
                pltpu.VMEM((1, steer.shape[0]), jnp.int32),
                pltpu.VMEM(kdir.shape, jnp.bfloat16),
                pltpu.VMEM(vdir.shape, jnp.bfloat16),
                pltpu.VMEM(keys.shape, jnp.bfloat16),
                pltpu.VMEM(values.shape, jnp.bfloat16),
                pltpu.VMEM((total_rows, 2 * kv_cols), jnp.bfloat16),
                pltpu.VMEM((rows, q_cols), jnp.bfloat16),
                pltpu.VMEM((rows, q_cols), jnp.bfloat16),
                pltpu.VMEM((total_rows, LANES), jnp.bfloat16),
                pltpu.VMEM((width, span), jnp.float32),
                pltpu.VMEM((width, span), jnp.bfloat16),
                pltpu.VMEM((kv_local, 2, width, LANES), jnp.float32),
                pltpu.VMEM((kv_local, width, 3 * LANES), jnp.float32),
                pltpu.VMEM((n + heads, 1, LANES), jnp.float32),
                dma((12,)),
                dma((n,)),
                dma((n,)),
                dma((n,)),
                dma((n,)),
                dma((n + heads,)),
                dma((n + heads,)),
            ],
            compiler_params=pltpu.CompilerParams(
                collective_id=0, has_side_effects=True, vmem_limit_bytes=48 * 1024 * 1024
            ),
        )(
            pltpu.with_memory_space_constraint(order, pltpu.HBM),
            strength,
            *(pltpu.with_memory_space_constraint(a, pltpu.HBM) for a in (
            steer.reshape(1, -1),
            kdir,
            vdir,
            keys,
            values,
            queries,
            target,))
        )
    )
    return tuple(
        pl.pallas_call(
            store,
            name="store",
            out_shape=tuple(
                jax.ShapeDtypeStruct(shape, kind)
                for shape, kind in (
                    ((rows, q_cols), jnp.bfloat16),
                    ((rows, q_cols), jnp.bfloat16),
                    ((1,), jnp.float32),
                )
            ),
            in_specs=[vm] * 3,
            compiler_params=pltpu.CompilerParams(vmem_limit_bytes=4 * 1024 * 1024),
            out_specs=(anywhere, anywhere, anywhere),
            scratch_shapes=[
                pltpu.VMEM((1,), jnp.float32),
                dma((3,)),
            ],
        )(*(pltpu.with_memory_space_constraint(o, pltpu.VMEM) for o in outs))
    )


def solution(mesh):
    wide = P(("rep", "seq"), "head")
    placed = (wide, wide, wide, P("head"), P("head"), P("rep"), P("rep"), P("rep"), wide)
    return jax.shard_map(
        body,
        mesh=mesh,
        in_specs=placed,
        out_specs=(wide, wide, P("rep")),
        check_vma=False,
    )
```

```python
import functools
import math

import jax
import jax.numpy as jnp
from jax import lax
from jax.experimental import pallas as pl
from jax.experimental.pallas import tpu as pltpu
from jax.sharding import PartitionSpec as P

HEAD_WIDTH = 128
MESH = pl.DeviceIdType.MESH
LANES = 128
MASKED = -1e30


def repeat(low, high, step):
    if high - low <= 16:
        for i in range(low, high):
            step(i)
    else:
        lax.fori_loop(low, high, lambda i, c: (step(i), c)[1], 0)


def kernel(
    n,
    heads,
    span,
    order_hbm,
    strength_hbm,
    steer_hbm,
    kdir_hbm,
    vdir_hbm,
    keys_hbm,
    values_hbm,
    queries_hbm,
    target_hbm,
    out_ref,
    tan_ref,
    sens_ref,
    order_ref,
    strength_ref,
    steer_ref,
    kdir_ref,
    vdir_ref,
    land_k,
    land_v,
    early_k,
    early_v,
    moved_k,
    moved_v,
    qbuf,
    tbuf,
    marks,
    score,
    weight,
    state,
    acc,
    parts,
    local_sem,
    k_send,
    k_recv,
    v_send,
    v_recv,
    part_send,
    part_recv,
    ready,
    entered,
):
    me = lax.axis_index("seq")
    my_head = lax.axis_index("head")
    rows, q_cols = qbuf.shape
    blk = rows // 2
    total_rows = land_k.shape[0]
    kv_cols = land_k.shape[1]
    kv_local = kv_cols // HEAD_WIDTH
    grouping = q_cols // HEAD_WIDTH // kv_local
    inverse = 1.0 / math.sqrt(HEAD_WIDTH)
    exponent = inverse * math.log2(math.e)
    chunks = total_rows // span

    barrier = pltpu.get_barrier_semaphore()

    side = lax.rem(me, 2)
    pair = me + 1 - 2 * side
    mate = 1 - 2 * side
    seat = me // 2
    seats = n // 2

    def greet(seq, head):
        pl.semaphore_signal(
            barrier, inc=1, device_id={"seq": seq, "head": head}, device_id_type=MESH
        )

    def greet_higher(k):
        @pl.when(seat + k < seats)
        def _():
            greet(me + 2 * k, my_head)

    @pl.when(side == 0)
    def _():
        greet(pair, my_head)

    repeat(1, seats, greet_higher)
    repeat(1, heads, lambda k: greet(me, lax.rem(my_head + k, heads)))

    own = pl.ds(pl.multiple_of(me * rows, rows), rows)
    fetched = []
    for i, (source, held) in enumerate(
        (
            (keys_hbm, land_k.at[own, :]),
            (values_hbm, land_v.at[own, :]),
            (order_hbm, order_ref),
            (steer_hbm, steer_ref),
            (strength_hbm, strength_ref),
            (kdir_hbm, kdir_ref),
            (vdir_hbm, vdir_ref),
            (queries_hbm, qbuf),
            (target_hbm, tbuf),
        )
    ):
        fetched.append(pltpu.make_async_copy(source, held, local_sem.at[i]))
        fetched[-1].start()
    q_copy, t_copy = fetched[7:]

    def copies(owner, device, lane, early, source):
        start = pl.ds(pl.multiple_of(owner * rows, rows), blk if early else rows)
        made = []
        for i, (land, sends, lands) in enumerate(
            ((land_k, k_send, k_recv), (land_v, v_send, v_recv))
        ):
            place = land.at[start, :]
            made.append(
                pltpu.make_async_remote_copy(
                    src_ref=place if source is None else source[i],
                    dst_ref=place,
                    send_sem=sends.at[lane],
                    recv_sem=lands.at[owner],
                    device_id={"seq": device},
                    device_id_type=MESH,
                )
            )
        return made

    whole_source = (keys_hbm, values_hbm)
    early_source = (early_k, early_v)

    def to_lower(peer):
        return copies(me, peer, peer, False, whole_source)

    def to_higher(peer):
        return copies(me, peer, peer, True, early_source)

    def start(made):
        for copy in made:
            copy.start()

    def outward(step):
        repeat(1, seats, step)

    def inward(step):
        repeat(1, seats, lambda i: step(seats - i))


    pl.semaphore_wait(barrier, seat + side + heads - 1)

    def admit(device):
        pl.semaphore_signal(
            entered.at[me], inc=1, device_id={"seq": device}, device_id_type=MESH
        )

    def admit_lower(k):
        @pl.when(seat >= k)
        def _():
            admit(me - 2 * k)

    inward(admit_lower)

    @pl.when(side == 1)
    def _():
        admit(pair)


    def down(k):
        @pl.when(seat >= k)
        def _():
            start(to_lower(me - 2 * k))

    inward(down)

    @pl.when(side == 1)
    def _():
        start(to_lower(pair))

    for copy in fetched[:3]:
        copy.wait()

    def block_of(owner, second):
        canonical = jnp.where(second == 1, 2 * n - 1 - owner, owner)
        return jnp.where(owner < me, canonical, order_ref[2 * owner + second])

    first_is_early = jnp.full((blk, kv_cols), order_ref[2 * me], jnp.int32) < n
    for land, early in ((land_k, early_k), (land_v, early_v)):
        held = land[own, :].astype(jnp.float32)
        early[...] = jnp.where(first_is_early, held[0:blk], held[blk:rows]).astype(jnp.bfloat16)

    def up(k):
        @pl.when(seat + k < seats)
        def _():
            pl.semaphore_wait(entered.at[me + 2 * k], 1)
            start(to_higher(me + 2 * k))

    @pl.when(side == 0)
    def _():
        pl.semaphore_wait(entered.at[pair], 1)
        start(to_higher(pair))

    outward(up)

    def clear(owner):
        @pl.when(owner < me)
        def _():
            late = pl.ds(pl.multiple_of(owner * rows + blk, blk), blk)
            land_k[late, :] = jnp.zeros((blk, kv_cols), land_k.dtype)
            land_v[late, :] = jnp.zeros((blk, kv_cols), land_v.dtype)

    repeat(0, n - 1, clear)

    for copy in fetched[3:7]:
        copy.wait()
    steer_count = steer_ref.shape[1]
    strength = strength_ref[0]

    def mark_rows(block):
        owner = block // 2
        number = block_of(owner, lax.rem(block, 2)) * blk
        place = number + lax.broadcasted_iota(jnp.int32, (blk, LANES), 0)
        hit = jnp.zeros((blk, LANES), jnp.float32)
        for c in range(0, steer_count, LANES):
            listed = steer_ref[:, c : c + LANES]
            hit = jnp.where(place == listed, 1.0, hit)
        found = jnp.max(hit, axis=1, keepdims=True)
        at = block * blk
        if not isinstance(at, int):
            at = pl.multiple_of(at, blk)
        marks[pl.ds(at, blk), :] = jnp.broadcast_to(found, (blk, LANES))

    repeat(0, 2 * n, mark_rows)

    row = lax.broadcasted_iota(jnp.int32, (rows, 1), 0)
    place = jnp.where(row < blk, order_ref[2 * me], order_ref[2 * me + 1]) * blk + lax.rem(row, blk)

    def key_places(c):
        lane = lax.broadcasted_iota(jnp.int32, (1, span), 1)
        block = lane // blk
        number = jnp.zeros((1, span), jnp.int32)
        for b in range(span // blk):
            index = c * (span // blk) + b
            number = jnp.where(block == b, block_of(index // 2, index % 2), number)
        return number * blk + lax.rem(lane, blk)

    q_copy.wait()
    coefs = []
    for g in range(kv_local):
        query = jnp.concatenate(
            [
                qbuf[:, (g * grouping + h) * LANES : (g * grouping + h + 1) * LANES]
                for h in range(grouping)
            ],
            axis=0,
        )
        spread = jnp.broadcast_to(kdir_ref[g * LANES : (g + 1) * LANES].reshape(1, LANES), (LANES, LANES))
        coef = lax.dot_general(
            query, spread, (((1,), (1,)), ((), ())), preferred_element_type=jnp.float32
        )
        coefs.append((query, coef * inverse))

    def pass_on(peer, early):
        made = copies(peer, pair, peer + mate, early, None)
        for copy in made:
            copy.wait_recv()
            copy.start()

    def take(owner, early):
        for copy in copies(owner, pair, pair, early, None):
            copy.wait_recv()

    def both(ranges, lower, higher):
        def near(k):
            @pl.when(seat >= k)
            def _():
                lower(me - 2 * k)

            @pl.when(seat + k < seats)
            def _():
                higher(me + 2 * k)

        ranges(near)

    both(inward, lambda p: pass_on(p, True), lambda p: pass_on(p, False))

    @pl.when(side == 1)
    def _():
        take(pair, True)

    @pl.when(side == 0)
    def _():
        take(pair, False)

    both(outward, lambda p: take(p + mate, True), lambda p: take(p + mate, False))
    repeat(
        1,
        heads,
        lambda k: pl.semaphore_signal(
            ready,
            inc=1,
            device_id={"seq": me, "head": lax.rem(my_head + k, heads)},
            device_id_type=MESH,
        ),
    )

    def shift(owner):
        at = owner * rows
        if not isinstance(at, int):
            at = pl.multiple_of(at, rows)
        here = pl.ds(at, rows)
        amount = strength * marks[here, 0:1]
        for land, moved, direction in ((land_k, moved_k, kdir_ref), (land_v, moved_v, vdir_ref)):
            step = direction[...].astype(jnp.float32).reshape(1, kv_cols)
            moved[here, :] = (land[here, :].astype(jnp.float32) + amount * step).astype(jnp.bfloat16)

    repeat(0, n, shift)

    def attend(g, c, start, fresh):
        query = coefs[g][0]
        cols = slice(g * LANES, (g + 1) * LANES)
        key = moved_k[pl.ds(start, span), cols]
        score[...] = lax.dot_general(
            query, key, (((1,), (1,)), ((), ())), preferred_element_type=jnp.float32
        )
        visible = key_places(c) <= place
        for h in range(grouping):
            part = slice(h * rows, (h + 1) * rows)
            scores = jnp.where(visible, score[part, :], MASKED)
            largest = jnp.max(scores, axis=1, keepdims=True)
            if not fresh:
                before = state[g, 0, part, :][:, 0:1]
                largest = jnp.maximum(before, largest)
            raw = jnp.exp2((scores - largest) * exponent)
            if not fresh:
                raw = jnp.where(visible, raw, 0.0)
            total = jnp.sum(raw, axis=1, keepdims=True)
            if not fresh:
                scale = jnp.exp2((before - largest) * exponent)
                total = total + scale * state[g, 1, part, :][:, 0:1]
                state[g, 0, part, :] = jnp.broadcast_to(largest, (rows, LANES))
                acc[g, part, :] = acc[g, part, :] * scale
            state[g, 1, part, :] = jnp.broadcast_to(total, (rows, LANES))
            weight[part, :] = raw.astype(jnp.bfloat16)
        mark = marks[pl.ds(start, span), :].astype(jnp.bfloat16)
        value = moved_v[pl.ds(start, span), cols]
        stacked = jnp.concatenate([value, value * mark, mark], axis=1)
        found = jnp.dot(weight[...], stacked, preferred_element_type=jnp.float32)
        if fresh:
            acc[g] = found
        else:
            acc[g] = acc[g] + found

    if chunks == 1:
        for g in range(kv_local):
            attend(g, 0, 0, True)
    else:
        state[:, 0] = jnp.full_like(state[:, 0], MASKED)
        state[:, 1] = jnp.zeros_like(state[:, 1])
        acc[...] = jnp.zeros_like(acc)

        def chunk(c, carry):
            for g in range(kv_local):
                attend(g, c, pl.multiple_of(c * span, span), False)
            return carry

        lax.fori_loop(0, chunks, chunk, 0)

    t_copy.wait()
    inner = jnp.zeros((rows, LANES), jnp.float32)
    for g in range(kv_local):
        direction = vdir_ref[g * LANES : (g + 1) * LANES].astype(jnp.float32).reshape(1, LANES)
        for h in range(grouping):
            part = slice(h * rows, (h + 1) * rows)
            lanes = slice((g * grouping + h) * LANES, (g * grouping + h + 1) * LANES)
            share = 1.0 / state[g, 1, part, :]
            primal = acc[g, part, 0:LANES] * share
            moment = acc[g, part, LANES : 2 * LANES]
            mass = acc[g, part, 2 * LANES : 3 * LANES]
            coef = coefs[g][1][part, :]
            deriv = (coef * (moment - mass * primal) + mass * direction) * share
            inner = inner + deriv * tbuf[:, lanes].astype(jnp.float32)
            out_ref[:, lanes] = primal.astype(jnp.bfloat16)
            tan_ref[:, lanes] = deriv.astype(jnp.bfloat16)

    mine = me * heads + my_head
    parts[mine] = jnp.sum(inner, axis=0, keepdims=True)
    pl.semaphore_wait(ready, heads - 1)

    def part_copy(seq, head, slot, lane):
        return pltpu.make_async_remote_copy(
            src_ref=parts.at[slot],
            dst_ref=parts.at[slot],
            send_sem=part_send.at[lane],
            recv_sem=part_recv.at[slot],
            device_id={"seq": seq, "head": head},
            device_id_type=MESH,
        )

    def other(i):
        to = lax.rem(mine + n * heads // 2 + i, n * heads)
        return to // heads, lax.rem(to, heads), to

    def part_out(i):
        seq, head, to = other(i)
        return part_copy(seq, head, mine, to)

    def part_in(i):
        seq, head, to = other(i)
        return part_copy(seq, head, to, to)

    def others(step):
        half = n * heads // 2
        repeat(0, half, step)
        repeat(half + 1, 2 * half, step)

    others(lambda i: part_out(i).start())
    others(lambda i: part_in(i).wait_recv())
    if n <= 16:
        whole = parts[0]
        for i in range(1, n * heads):
            whole = whole + parts[i]
    else:
        whole = lax.fori_loop(1, n * heads, lambda i, t: t + parts[i], parts[0])
    scale = 1.0 / math.sqrt(total_rows * q_cols * heads)
    sens_ref[...] = jnp.broadcast_to(jnp.sum(whole, axis=1, keepdims=True) * scale, (1, LANES))

    def finish(made):
        for copy in made:
            copy.wait_send()

    @pl.when(side == 0)
    def _():
        finish(to_higher(pair))

    @pl.when(side == 1)
    def _():
        finish(to_lower(pair))

    def lower_sent(peer):
        finish(to_lower(peer))
        finish(copies(peer, pair, peer + mate, True, None))

    def higher_sent(peer):
        finish(to_higher(peer))
        finish(copies(peer, pair, peer + mate, False, None))

    both(outward, lower_sent, higher_sent)
    others(lambda i: part_out(i).wait_send())


def store(primal, deriv, sens, primal_out, deriv_out, sens_out, one, sem):
    puts = [
        pltpu.make_async_copy(primal, primal_out, sem.at[0]),
        pltpu.make_async_copy(deriv, deriv_out, sem.at[1]),
        pltpu.make_async_copy(one, sens_out, sem.at[2]),
    ]
    puts[0].start()
    puts[1].start()
    one[...] = sens[0, 0:1]
    puts[2].start()
    for put in puts:
        put.wait()


def body(queries, keys, values, kdir, vdir, strength, order, steer, target):
    n = lax.axis_size("seq")
    heads = lax.axis_size("head")
    rows, q_cols = queries.shape
    kv_cols = keys.shape[1]
    kv_local = kv_cols // HEAD_WIDTH
    width = rows * (q_cols // kv_cols)
    total_rows = rows * n
    span = min(512, total_rows)
    anywhere = pl.BlockSpec(memory_space=pltpu.HBM)
    dma = pltpu.SemaphoreType.DMA
    near = pl.BlockSpec(memory_space=pltpu.VMEM)

    def far(array):
        return pltpu.with_memory_space_constraint(array, pltpu.HBM)

    outs = pl.pallas_call(
        functools.partial(kernel, n, heads, span),
        name="attend",
        out_shape=(
            pltpu.VMEM((rows, q_cols), jnp.bfloat16),
            pltpu.VMEM((rows, q_cols), jnp.bfloat16),
            pltpu.VMEM((1, LANES), jnp.float32),
        ),
        in_specs=[anywhere] * 9,
        out_specs=(near,) * 3,
        scratch_shapes=[
            pltpu.SMEM(order.shape, jnp.int32),
            pltpu.SMEM(strength.shape, jnp.float32),
            pltpu.VMEM((1, steer.shape[0]), jnp.int32),
            pltpu.VMEM(kdir.shape, jnp.bfloat16),
            pltpu.VMEM(vdir.shape, jnp.bfloat16),
            pltpu.VMEM((total_rows, kv_cols), jnp.bfloat16),
            pltpu.VMEM((total_rows, kv_cols), jnp.bfloat16),
            pltpu.VMEM((rows // 2, kv_cols), jnp.bfloat16),
            pltpu.VMEM((rows // 2, kv_cols), jnp.bfloat16),
            pltpu.VMEM((total_rows, kv_cols), jnp.bfloat16),
            pltpu.VMEM((total_rows, kv_cols), jnp.bfloat16),
            pltpu.VMEM((rows, q_cols), jnp.bfloat16),
            pltpu.VMEM((rows, q_cols), jnp.bfloat16),
            pltpu.VMEM((total_rows, LANES), jnp.float32),
            pltpu.VMEM((width, span), jnp.float32),
            pltpu.VMEM((width, span), jnp.bfloat16),
            pltpu.VMEM((kv_local, 2, width, LANES), jnp.float32),
            pltpu.VMEM((kv_local, width, 3 * LANES), jnp.float32),
            pltpu.VMEM((n * heads, 1, LANES), jnp.float32),
            dma((9,)),
            dma((n,)),
            dma((n,)),
            dma((n,)),
            dma((n,)),
            dma((n * heads,)),
            dma((n * heads,)),
            pltpu.SemaphoreType.REGULAR,
            pltpu.SemaphoreType.REGULAR((n,)),
        ],
        compiler_params=pltpu.CompilerParams(
            collective_id=0, has_side_effects=True, vmem_limit_bytes=48 * 1024 * 1024
        ),
    )(
        far(order),
        strength,
        far(steer.reshape(1, -1)),
        far(kdir),
        far(vdir),
        far(keys),
        far(values),
        far(queries),
        far(target),
    )
    return tuple(
        pl.pallas_call(
            store,
            name="store",
            out_shape=tuple(
                jax.ShapeDtypeStruct(shape, kind)
                for shape, kind in (
                    ((rows, q_cols), jnp.bfloat16),
                    ((rows, q_cols), jnp.bfloat16),
                    ((1,), jnp.float32),
                )
            ),
            in_specs=[near] * 3,
            out_specs=(anywhere,) * 3,
            scratch_shapes=[pltpu.VMEM((1,), jnp.float32), dma((3,))],
            compiler_params=pltpu.CompilerParams(vmem_limit_bytes=4 * 1024 * 1024),
        )(*(pltpu.with_memory_space_constraint(out, pltpu.VMEM) for out in outs))
    )


def solution(mesh):
    wide = P(("rep", "seq"), "head")
    placed = (wide, wide, wide, P("head"), P("head"), P("rep"), P("rep"), P("rep"), wide)
    return jax.shard_map(
        body,
        mesh=mesh,
        in_specs=placed,
        out_specs=(wide, wide, P("rep")),
        check_vma=False,
    )
```

```python
import functools
import math

import jax
import jax.numpy as jnp
from jax import lax
from jax.experimental import pallas as pl
from jax.experimental.pallas import tpu as pltpu
from jax.sharding import PartitionSpec as P

HEAD_WIDTH = 128
MESH = pl.DeviceIdType.MESH
LANES = 128
MASKED = -1e30


def repeat(low, high, step):
    if high - low <= 16:
        for i in range(low, high):
            step(i)
    else:
        lax.fori_loop(low, high, lambda i, c: (step(i), c)[1], 0)


def kernel(
    n,
    heads,
    span,
    order_hbm,
    strength_hbm,
    steer_hbm,
    kdir_hbm,
    vdir_hbm,
    keys_hbm,
    values_hbm,
    queries_hbm,
    target_hbm,
    out_ref,
    tan_ref,
    sens_ref,
    order_ref,
    strength_ref,
    steer_ref,
    kdir_ref,
    vdir_ref,
    land_k,
    land_v,
    early_k,
    early_v,
    moved_k,
    moved_v,
    qbuf,
    tbuf,
    marks,
    weight,
    state,
    acc,
    parts,
    local_sem,
    k_send,
    k_recv,
    v_send,
    v_recv,
    part_send,
    part_recv,
    ready,
    entered,
):
    me = lax.axis_index("seq")
    my_head = lax.axis_index("head")
    rows, q_cols = qbuf.shape
    blk = rows // 2
    total_rows = land_k.shape[0]
    kv_cols = land_k.shape[1]
    kv_local = kv_cols // HEAD_WIDTH
    grouping = q_cols // HEAD_WIDTH // kv_local
    inverse = 1.0 / math.sqrt(HEAD_WIDTH)
    exponent = inverse * math.log2(math.e)
    chunks = total_rows // span

    barrier = pltpu.get_barrier_semaphore()

    side = lax.rem(me, 2)
    pair = me + 1 - 2 * side
    mate = 1 - 2 * side
    seat = me // 2
    seats = n // 2

    def greet(seq, head):
        pl.semaphore_signal(
            barrier, inc=1, device_id={"seq": seq, "head": head}, device_id_type=MESH
        )

    def greet_higher(k):
        @pl.when(seat + k < seats)
        def _():
            greet(me + 2 * k, my_head)

    @pl.when(side == 0)
    def _():
        greet(pair, my_head)

    repeat(1, seats, greet_higher)
    repeat(1, heads, lambda k: greet(me, lax.rem(my_head + k, heads)))

    own = pl.ds(pl.multiple_of(seat * rows, rows), rows)
    fetched = []
    for i, (source, held) in enumerate(
        (
            (keys_hbm, land_k.at[own, :]),
            (values_hbm, land_v.at[own, :]),
            (order_hbm, order_ref),
            (steer_hbm, steer_ref),
            (strength_hbm, strength_ref),
            (kdir_hbm, kdir_ref),
            (vdir_hbm, vdir_ref),
            (queries_hbm, qbuf),
            (target_hbm, tbuf),
        )
    ):
        fetched.append(pltpu.make_async_copy(source, held, local_sem.at[i]))
        fetched[-1].start()
    q_copy, t_copy = fetched[7:]

    def copies(owner, device, lane, early, source, across):
        near_slot = owner // 2
        far_slot = near_slot + (seats if across else 0)
        count = blk if early else rows
        made = []
        for i, (land, sends, lands) in enumerate(
            ((land_k, k_send, k_recv), (land_v, v_send, v_recv))
        ):
            here = land.at[pl.ds(pl.multiple_of(near_slot * rows, rows), count), :]
            made.append(
                pltpu.make_async_remote_copy(
                    src_ref=here if source is None else source[i],
                    dst_ref=land.at[pl.ds(pl.multiple_of(far_slot * rows, rows), count), :],
                    send_sem=sends.at[lane],
                    recv_sem=lands.at[owner],
                    device_id={"seq": device},
                    device_id_type=MESH,
                )
            )
        return made

    whole_source = (keys_hbm, values_hbm)
    early_source = (early_k, early_v)

    def to_lower(peer, across=False):
        return copies(me, peer, peer, False, whole_source, across)

    def to_higher(peer, across=False):
        return copies(me, peer, peer, True, early_source, across)

    def start(made):
        for copy in made:
            copy.start()

    def outward(step):
        repeat(1, seats, step)

    def inward(step):
        repeat(1, seats, lambda i: step(seats - i))


    pl.semaphore_wait(barrier, seat + side + heads - 1)

    def admit(device):
        pl.semaphore_signal(
            entered.at[me], inc=1, device_id={"seq": device}, device_id_type=MESH
        )

    def admit_lower(k):
        @pl.when(seat >= k)
        def _():
            admit(me - 2 * k)

    inward(admit_lower)

    @pl.when(side == 1)
    def _():
        admit(pair)


    def down(k):
        @pl.when(seat >= k)
        def _():
            start(to_lower(me - 2 * k))

    @pl.when(side == 1)
    def _():
        start(to_lower(pair, True))

    inward(down)

    for copy in fetched[:3]:
        copy.wait()

    def owner_of(slot):
        return jnp.where(slot < seats, 2 * slot + side, 2 * (slot - seats) + 1 - side)

    def slot_of(owner):
        return jnp.where(lax.rem(owner, 2) == side, owner // 2, owner // 2 + seats)

    def block_of(index):
        owner = owner_of(index // 2)
        second = lax.rem(index, 2)
        canonical = jnp.where(second == 1, 2 * n - 1 - owner, owner)
        return jnp.where(owner < me, canonical, order_ref[2 * owner + second])

    first_is_early = jnp.full((blk, kv_cols), order_ref[2 * me], jnp.int32) < n
    for land, early in ((land_k, early_k), (land_v, early_v)):
        held = land[own, :].astype(jnp.float32)
        early[...] = jnp.where(first_is_early, held[0:blk], held[blk:rows]).astype(jnp.bfloat16)

    def up(k):
        @pl.when(seat + k < seats)
        def _():
            pl.semaphore_wait(entered.at[me + 2 * k], 1)
            start(to_higher(me + 2 * k))

    @pl.when(side == 0)
    def _():
        pl.semaphore_wait(entered.at[pair], 1)
        start(to_higher(pair, True))

    outward(up)

    def clear(owner):
        @pl.when(owner < me)
        def _():
            late = pl.ds(pl.multiple_of(slot_of(owner) * rows + blk, blk), blk)
            land_k[late, :] = jnp.zeros((blk, kv_cols), land_k.dtype)
            land_v[late, :] = jnp.zeros((blk, kv_cols), land_v.dtype)

    repeat(0, n - 1, clear)

    for copy in fetched[3:7]:
        copy.wait()
    steer_count = steer_ref.shape[1]
    strength = strength_ref[0]

    def mark_rows(block):
        number = block_of(block) * blk
        place = number + lax.broadcasted_iota(jnp.int32, (blk, LANES), 0)
        hit = jnp.zeros((blk, LANES), jnp.float32)
        for c in range(0, steer_count, LANES):
            listed = steer_ref[:, c : c + LANES]
            hit = jnp.where(place == listed, 1.0, hit)
        found = jnp.max(hit, axis=1, keepdims=True)
        at = block * blk
        if not isinstance(at, int):
            at = pl.multiple_of(at, blk)
        marks[pl.ds(at, blk), :] = jnp.broadcast_to(found, (blk, LANES))

    repeat(0, 2 * n, mark_rows)

    row = lax.broadcasted_iota(jnp.int32, (rows, 1), 0)
    place = jnp.where(row < blk, order_ref[2 * me], order_ref[2 * me + 1]) * blk + lax.rem(row, blk)

    def key_places(c):
        lane = lax.broadcasted_iota(jnp.int32, (1, span), 1)
        block = lane // blk
        number = jnp.zeros((1, span), jnp.int32)
        for b in range(span // blk):
            index = c * (span // blk) + b
            number = jnp.where(block == b, block_of(index), number)
        return number * blk + lax.rem(lane, blk)

    q_copy.wait()
    coefs = []
    for g in range(kv_local):
        query = jnp.concatenate(
            [
                qbuf[:, (g * grouping + h) * LANES : (g * grouping + h + 1) * LANES]
                for h in range(grouping)
            ],
            axis=0,
        )
        spread = jnp.broadcast_to(kdir_ref[g * LANES : (g + 1) * LANES].reshape(1, LANES), (LANES, LANES))
        coef = lax.dot_general(
            query, spread, (((1,), (1,)), ((), ())), preferred_element_type=jnp.float32
        )
        coefs.append((query, coef * inverse))

    def pass_on(peer, early):
        made = copies(peer, pair, peer + mate, early, None, True)
        for copy in made:
            copy.wait_recv()
            copy.start()

    def take(owner, early):
        for copy in copies(owner, pair, pair, early, None, True):
            copy.wait_recv()

    def both(ranges, lower, higher):
        def near(k):
            @pl.when(seat >= k)
            def _():
                lower(me - 2 * k)

            @pl.when(seat + k < seats)
            def _():
                higher(me + 2 * k)

        ranges(near)

    both(inward, lambda p: pass_on(p, True), lambda p: pass_on(p, False))

    def shift(slot):
        at = slot * rows
        if not isinstance(at, int):
            at = pl.multiple_of(at, rows)
        here = pl.ds(at, rows)
        amount = strength * marks[here, 0:1]
        for land, moved, direction in ((land_k, moved_k, kdir_ref), (land_v, moved_v, vdir_ref)):
            step = direction[...].astype(jnp.float32).reshape(1, kv_cols)
            moved[here, :] = (land[here, :].astype(jnp.float32) + amount * step).astype(jnp.bfloat16)

    def facts(c, start):
        marked = lax.dot_general(
            jnp.full((8, LANES), 1.0 / LANES, jnp.bfloat16),
            marks[pl.ds(start, span), :].astype(jnp.bfloat16),
            (((1,), (1,)), ((), ())),
            preferred_element_type=jnp.float32,
        )[0:1, :]
        return key_places(c) <= place, marked

    known = [facts(c, c * span) for c in range(2)] if chunks == 2 else None

    def attend(which, g, c, start, fresh, guarded):
        query = coefs[g][0]
        cols = slice(g * LANES, (g + 1) * LANES)
        key = moved_k[pl.ds(start, span), cols]
        found_score = lax.dot_general(
            query, key, (((1,), (1,)), ((), ())), preferred_element_type=jnp.float32
        )
        visible, marked = known[c] if chunks == 2 else facts(c, start)
        for h in range(grouping):
            part = slice(h * rows, (h + 1) * rows)
            scores = jnp.where(visible, found_score[part, :], MASKED)
            largest = jnp.max(scores, axis=1, keepdims=True)
            if not fresh:
                before = state[which, g, 0, part, :][:, 0:1]
                largest = jnp.maximum(before, largest)
            raw = jnp.exp2((scores - largest) * exponent)
            if guarded:
                raw = jnp.where(visible, raw, 0.0)
            total = jnp.sum(raw, axis=1, keepdims=True)
            if not fresh:
                scale = jnp.exp2((before - largest) * exponent)
                total = total + scale * state[which, g, 1, part, :][:, 0:1]
                acc[which, g, part, :] = acc[which, g, part, :] * scale
            state[which, g, 0, part, :] = jnp.broadcast_to(largest, (rows, LANES))
            state[which, g, 1, part, :] = jnp.broadcast_to(total, (rows, LANES))
            rounded = raw.astype(jnp.bfloat16)
            mass = jnp.sum(rounded.astype(jnp.float32) * marked, axis=1, keepdims=True)
            if not fresh:
                mass = mass + scale * state[which, g, 2, part, :][:, 0:1]
            state[which, g, 2, part, :] = jnp.broadcast_to(mass, (rows, LANES))
            weight[g, part, :] = rounded
        mark = marks[pl.ds(start, span), :].astype(jnp.bfloat16)
        value = moved_v[pl.ds(start, span), cols]
        stacked = jnp.concatenate([value, value * mark], axis=1)
        found = jnp.dot(weight[g], stacked, preferred_element_type=jnp.float32)
        if fresh:
            acc[which, g] = found
        else:
            acc[which, g] = acc[which, g] + found

    def half(which):
        repeat(which * seats, (which + 1) * seats, shift)
        if chunks == 2:
            for g in range(kv_local):
                attend(which, g, which, which * span, True, False)
        else:

            def chunk(c, carry):
                for g in range(kv_local):
                    attend(which, g, c, pl.multiple_of(c * span, span), False, True)
                return carry

            lax.fori_loop(which * (chunks // 2), (which + 1) * (chunks // 2), chunk, 0)

    if chunks > 2:
        state[:, :, 0] = jnp.full_like(state[:, :, 0], MASKED)
        state[:, :, 1:3] = jnp.zeros_like(state[:, :, 1:3])
        acc[...] = jnp.zeros_like(acc)

    half(0)

    @pl.when(side == 1)
    def _():
        take(pair, True)

    @pl.when(side == 0)
    def _():
        take(pair, False)

    both(outward, lambda p: take(p + mate, True), lambda p: take(p + mate, False))
    repeat(
        1,
        heads,
        lambda k: pl.semaphore_signal(
            ready,
            inc=1,
            device_id={"seq": me, "head": lax.rem(my_head + k, heads)},
            device_id_type=MESH,
        ),
    )

    half(1)

    t_copy.wait()
    inner = jnp.zeros((rows, LANES), jnp.float32)
    for g in range(kv_local):
        direction = vdir_ref[g * LANES : (g + 1) * LANES].astype(jnp.float32).reshape(1, LANES)
        for h in range(grouping):
            part = slice(h * rows, (h + 1) * rows)
            lanes = slice((g * grouping + h) * LANES, (g * grouping + h + 1) * LANES)
            first, second = state[0, g, 0, part, :], state[1, g, 0, part, :]
            largest = jnp.maximum(first, second)
            first = jnp.exp2((first - largest) * exponent)
            second = jnp.exp2((second - largest) * exponent)
            share = 1.0 / (first * state[0, g, 1, part, :] + second * state[1, g, 1, part, :])
            first, second = first * share, second * share
            primal, moment = (
                first * acc[0, g, part, i * LANES : (i + 1) * LANES]
                + second * acc[1, g, part, i * LANES : (i + 1) * LANES]
                for i in range(2)
            )
            mass = first * state[0, g, 2, part, :] + second * state[1, g, 2, part, :]
            coef = coefs[g][1][part, :]
            deriv = coef * (moment - mass * primal) + mass * direction
            inner = inner + deriv * tbuf[:, lanes].astype(jnp.float32)
            out_ref[:, lanes] = primal.astype(jnp.bfloat16)
            tan_ref[:, lanes] = deriv.astype(jnp.bfloat16)

    mine = me * heads + my_head
    parts[mine] = jnp.sum(inner, axis=0, keepdims=True)
    pl.semaphore_wait(ready, heads - 1)

    def part_copy(seq, head, slot, lane):
        return pltpu.make_async_remote_copy(
            src_ref=parts.at[slot],
            dst_ref=parts.at[slot],
            send_sem=part_send.at[lane],
            recv_sem=part_recv.at[slot],
            device_id={"seq": seq, "head": head},
            device_id_type=MESH,
        )

    def other(i):
        to = lax.rem(mine + n * heads // 2 + i, n * heads)
        return to // heads, lax.rem(to, heads), to

    def part_out(i):
        seq, head, to = other(i)
        return part_copy(seq, head, mine, to)

    def part_in(i):
        seq, head, to = other(i)
        return part_copy(seq, head, to, to)

    def others(step):
        half = n * heads // 2
        repeat(0, half, step)
        repeat(half + 1, 2 * half, step)

    others(lambda i: part_out(i).start())
    others(lambda i: part_in(i).wait_recv())
    if n <= 16:
        whole = parts[0]
        for i in range(1, n * heads):
            whole = whole + parts[i]
    else:
        whole = lax.fori_loop(1, n * heads, lambda i, t: t + parts[i], parts[0])
    scale = 1.0 / math.sqrt(total_rows * q_cols * heads)
    sens_ref[...] = jnp.broadcast_to(jnp.sum(whole, axis=1, keepdims=True) * scale, (1, LANES))

    def finish(made):
        for copy in made:
            copy.wait_send()

    @pl.when(side == 0)
    def _():
        finish(to_higher(pair, True))

    @pl.when(side == 1)
    def _():
        finish(to_lower(pair, True))

    def lower_sent(peer):
        finish(to_lower(peer))
        finish(copies(peer, pair, peer + mate, True, None, True))

    def higher_sent(peer):
        finish(to_higher(peer))
        finish(copies(peer, pair, peer + mate, False, None, True))

    both(outward, lower_sent, higher_sent)
    others(lambda i: part_out(i).wait_send())


def store(primal, deriv, sens, primal_out, deriv_out, sens_out, one, sem):
    puts = [
        pltpu.make_async_copy(primal, primal_out, sem.at[0]),
        pltpu.make_async_copy(deriv, deriv_out, sem.at[1]),
        pltpu.make_async_copy(one, sens_out, sem.at[2]),
    ]
    puts[0].start()
    puts[1].start()
    one[...] = sens[0, 0:1]
    puts[2].start()
    for put in puts:
        put.wait()


def body(queries, keys, values, kdir, vdir, strength, order, steer, target):
    n = lax.axis_size("seq")
    heads = lax.axis_size("head")
    rows, q_cols = queries.shape
    kv_cols = keys.shape[1]
    kv_local = kv_cols // HEAD_WIDTH
    width = rows * (q_cols // kv_cols)
    total_rows = rows * n
    span = min(512, total_rows // 2)
    anywhere = pl.BlockSpec(memory_space=pltpu.HBM)
    dma = pltpu.SemaphoreType.DMA
    near = pl.BlockSpec(memory_space=pltpu.VMEM)

    def far(array):
        return pltpu.with_memory_space_constraint(array, pltpu.HBM)

    outs = pl.pallas_call(
        functools.partial(kernel, n, heads, span),
        name="attend",
        out_shape=(
            pltpu.VMEM((rows, q_cols), jnp.bfloat16),
            pltpu.VMEM((rows, q_cols), jnp.bfloat16),
            pltpu.VMEM((1, LANES), jnp.float32),
        ),
        in_specs=[anywhere] * 9,
        out_specs=(near,) * 3,
        scratch_shapes=[
            pltpu.SMEM(order.shape, jnp.int32),
            pltpu.SMEM(strength.shape, jnp.float32),
            pltpu.VMEM((1, steer.shape[0]), jnp.int32),
            pltpu.VMEM(kdir.shape, jnp.bfloat16),
            pltpu.VMEM(vdir.shape, jnp.bfloat16),
            pltpu.VMEM((total_rows, kv_cols), jnp.bfloat16),
            pltpu.VMEM((total_rows, kv_cols), jnp.bfloat16),
            pltpu.VMEM((rows // 2, kv_cols), jnp.bfloat16),
            pltpu.VMEM((rows // 2, kv_cols), jnp.bfloat16),
            pltpu.VMEM((total_rows, kv_cols), jnp.bfloat16),
            pltpu.VMEM((total_rows, kv_cols), jnp.bfloat16),
            pltpu.VMEM((rows, q_cols), jnp.bfloat16),
            pltpu.VMEM((rows, q_cols), jnp.bfloat16),
            pltpu.VMEM((total_rows, LANES), jnp.float32),
            pltpu.VMEM((kv_local, width, span), jnp.bfloat16),
            pltpu.VMEM((2, kv_local, 3, width, LANES), jnp.float32),
            pltpu.VMEM((2, kv_local, width, 2 * LANES), jnp.float32),
            pltpu.VMEM((n * heads, 1, LANES), jnp.float32),
            dma((9,)),
            dma((n,)),
            dma((n,)),
            dma((n,)),
            dma((n,)),
            dma((n * heads,)),
            dma((n * heads,)),
            pltpu.SemaphoreType.REGULAR,
            pltpu.SemaphoreType.REGULAR((n,)),
        ],
        compiler_params=pltpu.CompilerParams(
            collective_id=0, has_side_effects=True, vmem_limit_bytes=48 * 1024 * 1024
        ),
    )(
        far(order),
        strength,
        far(steer.reshape(1, -1)),
        far(kdir),
        far(vdir),
        far(keys),
        far(values),
        far(queries),
        far(target),
    )
    return tuple(
        pl.pallas_call(
            store,
            name="store",
            out_shape=tuple(
                jax.ShapeDtypeStruct(shape, kind)
                for shape, kind in (
                    ((rows, q_cols), jnp.bfloat16),
                    ((rows, q_cols), jnp.bfloat16),
                    ((1,), jnp.float32),
                )
            ),
            in_specs=[near] * 3,
            out_specs=(anywhere,) * 3,
            scratch_shapes=[pltpu.VMEM((1,), jnp.float32), dma((3,))],
            compiler_params=pltpu.CompilerParams(vmem_limit_bytes=4 * 1024 * 1024),
        )(*(pltpu.with_memory_space_constraint(out, pltpu.VMEM) for out in outs))
    )


def solution(mesh):
    wide = P(("rep", "seq"), "head")
    placed = (wide, wide, wide, P("head"), P("head"), P("rep"), P("rep"), P("rep"), wide)
    return jax.shard_map(
        body,
        mesh=mesh,
        in_specs=placed,
        out_specs=(wide, wide, P("rep")),
        check_vma=False,
    )
```
